32 devices in a mesh: row: 16 (over z, x, core), col: 2 (over y).
Axes of the slice: x: 2, y: 2, z: 4, core: 2. Of those that a mesh axis runs over, the one named last changes fastest.
Arguments:
- dosage: bfloat16 [128, 24576], P(('row', 'col')), may hold values from 0 to 2
- phenos: bfloat16 [16, 24576], P(None, 'col'), may hold values from -6 to 6
Outputs:
- grm: float32 [24576, 24576], P('row', 'col')
- projected: float32 [16, 24576], P(None, ('row', 'col'))
The draws below stay inside these ranges and needn't reach their ends.
All inputs are finite; a program needn't handle non-finite values.
Results may differ from the reference program's by a relative error of at most 0.0049.
Values may be sent and summed in bfloat16 or wider, within the bound.
A program may use at most 192 MiB of HBM per device.

```python
import math
import jax
import jax.numpy as jnp
from jax import lax

SAMPLES = 24576
PHENOS = 16
SNPS = 128


def draw_dosage(key, part):
    key_freq, key_unif = jax.random.split(key, 2)
    freq = jnp.exp(jax.random.uniform(key_freq, (SNPS, 1), jnp.float32, math.log(0.05), math.log(0.5)))
    unif = jax.random.uniform(key_unif, (SNPS, SAMPLES), jnp.float32)
    return (4.0 * freq * unif).astype(jnp.bfloat16)


def block_scale(own_key, dims, cuts, smallest, largest):
    loudness, own = 1.0, jax.random.fold_in(own_key, 6)
    for position, parts in cuts:
        heights = jnp.exp(jax.random.uniform(jax.random.fold_in(own, position), (parts,), jnp.float32, smallest / len(cuts), largest / len(cuts)))
        loudness = loudness * jnp.repeat(heights, dims[position] // parts).reshape([-1 if axis == position else 1 for axis in range(len(dims))])
    return loudness


def gaussian(key, shape, scale, bound, cuts=(), kind=jnp.bfloat16):
    level = block_scale(key, shape, cuts, -0.22, 0.18) if cuts else 1.0
    values = jax.random.normal(key, shape, jnp.float32) * scale * level
    return jnp.minimum(jnp.maximum(values, -bound), bound).astype(kind)


def setup_inputs(seed: int = 0) -> dict:
    arg_keys = jax.random.split(jax.random.key(seed), 3)
    return {
        "dosage": draw_dosage(jax.random.fold_in(arg_keys[2], 71), 0),
        "phenos": gaussian(arg_keys[1], (PHENOS, SAMPLES), 1.0, 6.0, ((1, 2),)),
    }


eps = 1e-05

def standardize(dosage):
    values = dosage.astype(jnp.float32)
    site_mean = lax.optimization_barrier(jnp.mean(values, axis=1, keepdims=True))
    centred = values - site_mean
    site_var = lax.optimization_barrier(jnp.mean(centred * centred, axis=1, keepdims=True))
    return (centred * lax.rsqrt(site_var + eps)).astype(jnp.bfloat16)

def reference(dosage, phenos):
    standard = standardize(dosage)
    grm = jnp.dot(standard.T, standard, preferred_element_type=jnp.float32) * (1.0 / SNPS)
    grm_half = grm.astype(jnp.bfloat16)
    projected = lax.dot_general(phenos, grm_half, (((1,), (1,)), ((), ())), preferred_element_type=jnp.float32)
    return (grm, projected)
```

```python
import functools

import jax
import jax.numpy as jnp
from jax import lax
from jax.experimental import pallas as pl
from jax.experimental.pallas import tpu as pltpu
from jax.sharding import PartitionSpec as P

eps = 1e-05
MESH = pl.DeviceIdType.MESH


def place_of(row, depth, width):
    chip, core = row // 2, row % 2
    a, b = chip // width, chip % width
    turn = depth - 1 - a
    odd = turn % 2
    first = (width - 1 - b) // (width - 1)
    later = depth + turn * (width - 1) + (1 - odd) * (b - 1) + odd * (width - 1 - b)
    return first * a + (1 - first) * later, core


def row_at(place, core, depth, width):
    first = 1 - jnp.minimum(place // depth, 1)
    rest = jnp.maximum(place - depth, 0)
    turn, step = rest // (width - 1), rest % (width - 1)
    odd = turn % 2
    later = (depth - 1 - turn) * width + (1 - odd) * (1 + step) + odd * (width - 1 - step)
    return (first * place * width + (1 - first) * later) * 2 + core


def gather_kernel(
    rows, cols, dosage_ref, phenos_ref, col_ref, row_ref, weight_ref,
    mine, swapped, parts, swap_send, swap_recv, ring_send, ring_recv, sib_send, sib_recv,
    line_send, line_recv, part_send, part_recv,
):
    row, col = lax.axis_index("row"), lax.axis_index("col")
    chips = rows // 2
    depth = min(4, chips)
    width = chips // depth
    place, core = place_of(row, depth, width)
    sibling = row + 1 - 2 * core
    ahead = row_at((place + 1) % chips, core, depth, width)
    behind = row_at((place + chips - 1) % chips, core, depth, width)
    sites = dosage_ref.shape[0]
    wide = col_ref.shape[2]
    half = wide // 2
    tall = row_ref.shape[2]
    per_col = rows // cols
    home = row // per_col
    offset = pl.multiple_of((row % per_col) * tall, 128)

    barrier = pltpu.get_barrier_semaphore()
    for other in (ahead, behind, sibling):
        pl.semaphore_signal(barrier, inc=1, device_id=(other, col), device_id_type=MESH)
    for k in range(1, cols):
        pl.semaphore_signal(
            barrier, inc=1, device_id=(row, (col + k) % cols), device_id_type=MESH
        )

    values = dosage_ref[...].astype(jnp.float32)
    samples = values.shape[1]
    mean = jnp.sum(values, axis=1, keepdims=True) * (1.0 / samples)
    centred = values - mean
    var = jnp.sum(centred * centred, axis=1, keepdims=True) * (1.0 / samples)
    scale = lax.rsqrt(var + eps)
    for c in range(cols):
        piece = dosage_ref[:, c * wide:(c + 1) * wide].astype(jnp.float32)
        mine[c] = ((piece - mean) * scale).astype(jnp.bfloat16)

    pl.semaphore_wait(barrier, 3 + cols - 1)

    swaps = []
    for k in range(1, cols):
        target = (col + k) % cols
        swap = pltpu.make_async_remote_copy(
            src_ref=mine.at[target], dst_ref=swapped.at[col],
            send_sem=swap_send.at[k - 1], recv_sem=swap_recv.at[k - 1],
            device_id=(row, target), device_id_type=MESH,
        )
        swap.start()
        swaps.append(swap)
    swapped[col] = mine[col]
    for swap in swaps:
        swap.wait_recv()
    for c in range(cols):
        col_ref[row, c * sites:(c + 1) * sites, :] = swapped[c]

    def ring_copy(direction, step, part, source):
        lane = pl.ds(part * half, half)
        target = ahead if direction == 0 else behind
        where = col_ref.at[source, :, lane]
        return pltpu.make_async_remote_copy(
            src_ref=where, dst_ref=where,
            send_sem=ring_send.at[direction, step, part],
            recv_sem=ring_recv.at[direction, step, part],
            device_id=(target, col), device_id_type=MESH,
        )

    def sib_copy(index, source):
        where = col_ref.at[source]
        return pltpu.make_async_remote_copy(
            src_ref=where, dst_ref=where,
            send_sem=sib_send.at[index], recv_sem=sib_recv.at[index],
            device_id=(sibling, col), device_id_type=MESH,
        )

    def line_copy(source, k):
        return pltpu.make_async_remote_copy(
            src_ref=col_ref.at[source, :, pl.ds(offset, tall)], dst_ref=row_ref.at[source],
            send_sem=line_send.at[source, k - 1], recv_sem=line_recv.at[source],
            device_id=(row, (col + k) % cols), device_id_type=MESH,
        )

    def lines(source):
        @pl.when(home == col)
        def _():
            for k in range(1, cols):
                line_copy(source, k).start()
            row_ref[source] = col_ref[source, :, pl.ds(offset, tall)]

    steps = chips // 2
    sent = []

    def launch(copy):
        copy.start()
        sent.append(copy)

    def routes(step):
        if step < steps - 1:
            return [(0, 0), (1, 1), (0, 1), (1, 0)]
        return [(0, 0), (1, 1)]

    for direction, part in routes(0):
        launch(ring_copy(direction, 0, part, row))
    launch(sib_copy(0, row))
    lines(row)
    waiting = [(0, sibling)]
    count = 1
    for step in range(steps):
        sources = (
            row_at((place + 2 * chips - step - 1) % chips, core, depth, width),
            row_at((place + step + 1) % chips, core, depth, width),
        )
        for direction, part in routes(step):
            ring_copy(direction, step, part, sources[direction]).wait_recv()
            if step + 1 < steps and (direction, part) in routes(step + 1):
                launch(ring_copy(direction, step + 1, part, sources[direction]))
        for source in sources if step < steps - 1 else sources[:1]:
            launch(sib_copy(count, source))
            lines(source)
            waiting.append((count, source + 1 - 2 * core))
            count += 1
        due = waiting[:-2] if step < steps - 1 else waiting
        waiting = waiting[len(due):]
        for index, source in due:
            sib_copy(index, source).wait_recv()
            lines(source)

    block = col_ref.shape[1]
    product = lax.dot_general(
        phenos_ref[...], col_ref[...].reshape(rows * block, wide),
        (((1,), (1,)), ((), ())), preferred_element_type=jnp.float32,
    )
    parts[0] = product
    trades = []
    for k in range(1, cols):
        trade = pltpu.make_async_remote_copy(
            src_ref=parts.at[0], dst_ref=parts.at[k],
            send_sem=part_send.at[k - 1], recv_sem=part_recv.at[k - 1],
            device_id=(row, (col + k) % cols), device_id_type=MESH,
        )
        trade.start()
        trades.append(trade)

    @pl.when(home != col)
    def _():
        def take(source, carry):
            line_copy(source, 1).wait_recv()
            return carry
        lax.fori_loop(0, rows, take, 0)

    @pl.when(home == col)
    def _():
        def take(source, carry):
            for k in range(1, cols):
                line_copy(source, k).wait_send()
            return carry
        lax.fori_loop(0, rows, take, 0)

    total = parts[0]
    for k in range(1, cols):
        trades[k - 1].wait_recv()
        total = total + parts[k]
    weight_ref[...] = total
    for copy in swaps + sent + trades:
        copy.wait_send()


def product_kernel(cols, row_ref, col_ref, weight_ref, grm_ref, projected_ref):
    sites = row_ref.shape[0]

    @pl.when(pl.program_id(0) == 0)
    def _():
        part = projected_ref.shape[1]
        col = lax.axis_index("col")
        lane = pl.ds(pl.multiple_of(col * part, 128), part)
        projected_ref[...] = jnp.dot(
            weight_ref[...], row_ref[:, lane].astype(jnp.float32),
            precision=lax.Precision.HIGHEST, preferred_element_type=jnp.float32,
        ) * (1.0 / sites)

    tall = grm_ref.shape[0]
    lines = pl.ds(pl.multiple_of(pl.program_id(0) * tall, 128), tall)
    grm_ref[...] = lax.dot_general(
        row_ref[:, lines], col_ref[...], (((0,), (0,)), ((), ())),
        preferred_element_type=jnp.float32,
    ) * (1.0 / sites)


def per_device(rows, cols, dosage, phenos):
    sites, samples = dosage.shape
    count = phenos.shape[0]
    block, wide, tall = sites * cols, samples // cols, samples // rows
    total = rows * block
    vmem = pl.BlockSpec(memory_space=pltpu.VMEM)
    dma = pltpu.SemaphoreType.DMA
    chips = rows // 2
    others = cols - 1
    col_block, row_block, weight = pl.pallas_call(
        functools.partial(gather_kernel, rows, cols),
        out_shape=[
            jax.ShapeDtypeStruct((rows, block, wide), jnp.bfloat16),
            jax.ShapeDtypeStruct((rows, block, tall), jnp.bfloat16),
            jax.ShapeDtypeStruct((count, total), jnp.float32),
        ],
        in_specs=[vmem, vmem],
        out_specs=[vmem, vmem, vmem],
        scratch_shapes=[
            pltpu.VMEM((cols, sites, wide), jnp.bfloat16),
            pltpu.VMEM((cols, sites, wide), jnp.bfloat16),
            pltpu.VMEM((cols, count, total), jnp.float32),
            dma((others,)), dma((others,)),
            dma((2, chips // 2, 2)), dma((2, chips // 2, 2)),
            dma((chips,)), dma((chips,)),
            dma((rows, others)), dma((rows,)),
            dma((others,)), dma((others,)),
        ],
        compiler_params=pltpu.CompilerParams(
            collective_id=0, has_side_effects=True, vmem_limit_bytes=48 * 2**20
        ),
        name="gather",
    )(dosage, phenos)
    row_block = row_block.reshape(total, tall)
    col_block = col_block.reshape(total, wide)
    lines = 128
    grm, projected = pl.pallas_call(
        functools.partial(product_kernel, cols),
        grid=(tall // lines,),
        out_shape=[
            jax.ShapeDtypeStruct((tall, wide), jnp.float32),
            jax.ShapeDtypeStruct((count, tall // cols), jnp.float32),
        ],
        in_specs=[vmem, vmem, vmem],
        out_specs=[
            pl.BlockSpec((lines, wide), lambda i: (i, 0)),
            pl.BlockSpec((count, tall // cols), lambda i: (0, 0)),
        ],
        compiler_params=pltpu.CompilerParams(vmem_limit_bytes=48 * 2**20),
        name="product",
    )(row_block, col_block, weight)
    return grm, projected


def solution(mesh):
    rows, cols = mesh.shape["row"], mesh.shape["col"]
    return jax.shard_map(
        functools.partial(per_device, rows, cols),
        mesh=mesh,
        in_specs=(P(("row", "col"), None), P(None, "col")),
        out_specs=(P("row", "col"), P(None, ("row", "col"))),
        check_vma=False,
    )
```

```python
import functools

import jax
import jax.numpy as jnp
from jax import lax
from jax.experimental import pallas as pl
from jax.experimental.pallas import tpu as pltpu
from jax.sharding import PartitionSpec as P

eps = 1e-05
MESH = pl.DeviceIdType.MESH


def place_of(row, depth, width):
    chip, core = row // 2, row % 2
    a, b = chip // width, chip % width
    turn = depth - 1 - a
    odd = turn % 2
    first = (width - 1 - b) // (width - 1)
    later = depth + turn * (width - 1) + (1 - odd) * (b - 1) + odd * (width - 1 - b)
    return first * a + (1 - first) * later, core


def row_at(place, core, depth, width):
    first = 1 - jnp.minimum(place // depth, 1)
    rest = jnp.maximum(place - depth, 0)
    turn, step = rest // (width - 1), rest % (width - 1)
    odd = turn % 2
    later = (depth - 1 - turn) * width + (1 - odd) * (1 + step) + odd * (width - 1 - step)
    return (first * place * width + (1 - first) * later) * 2 + core


def gather_kernel(
    rows, cols, dosage_ref, phenos_ref, col_ref, row_ref, weight_ref,
    mine, pieces, parts, swap_send, swap_recv, ring_send, ring_recv, sib_send, sib_recv,
    line_send, line_recv, part_send, part_recv,
):
    row, col = lax.axis_index("row"), lax.axis_index("col")
    chips = rows // 2
    depth = min(4, chips)
    width = chips // depth
    place, core = place_of(row, depth, width)
    sibling = row + 1 - 2 * core
    ahead = row_at((place + 1) % chips, core, depth, width)
    behind = row_at((place + chips - 1) % chips, core, depth, width)
    sites = dosage_ref.shape[0]
    wide = col_ref.shape[2]
    tall = row_ref.shape[2]
    per_col = rows // cols
    home = row // per_col
    offset = pl.multiple_of((row % per_col) * tall, 128)

    barrier = pltpu.get_barrier_semaphore()
    for other in (ahead, behind, sibling):
        pl.semaphore_signal(barrier, inc=1, device_id=(other, col), device_id_type=MESH)
    for k in range(1, cols):
        pl.semaphore_signal(
            barrier, inc=1, device_id=(row, (col + k) % cols), device_id_type=MESH
        )

    values = dosage_ref[...].astype(jnp.float32)
    samples = values.shape[1]
    mean = jnp.sum(values, axis=1, keepdims=True) * (1.0 / samples)
    centred = values - mean
    var = jnp.sum(centred * centred, axis=1, keepdims=True) * (1.0 / samples)
    scale = lax.rsqrt(var + eps)

    def standard(c):
        lane = pl.ds(pl.multiple_of(c * wide, 128), wide)
        piece = dosage_ref[:, lane].astype(jnp.float32)
        return ((piece - mean) * scale).astype(jnp.bfloat16)

    steps = chips // 2
    sent = []

    def launch(copy):
        copy.start()
        sent.append(copy)

    swaps = []
    for k in range(1, cols):
        target = (col + k) % cols
        mine[k - 1] = standard(target)
        if k == 1:
            pl.semaphore_wait(barrier, 3 + cols - 1)
        swap = pltpu.make_async_remote_copy(
            src_ref=mine.at[k - 1], dst_ref=pieces.at[row, col],
            send_sem=swap_send.at[k - 1], recv_sem=swap_recv.at[k - 1],
            device_id=(row, target), device_id_type=MESH,
        )
        launch(swap)
        swaps.append(swap)

    def ring_copy(direction, step, k, source):
        target = ahead if direction == 0 else behind
        where = pieces.at[source, (col + cols - k) % cols]
        return pltpu.make_async_remote_copy(
            src_ref=where, dst_ref=where,
            send_sem=ring_send.at[direction, step, k],
            recv_sem=ring_recv.at[direction, step, k],
            device_id=(target, col), device_id_type=MESH,
        )

    def assemble(source):
        for c in range(cols):
            col_ref[source, c * sites:(c + 1) * sites, :] = pieces[source, c]

    def sib_copy(index, source):
        where = col_ref.at[source]
        return pltpu.make_async_remote_copy(
            src_ref=where, dst_ref=where,
            send_sem=sib_send.at[index], recv_sem=sib_recv.at[index],
            device_id=(sibling, col), device_id_type=MESH,
        )

    def line_copy(source, k):
        return pltpu.make_async_remote_copy(
            src_ref=col_ref.at[source, :, pl.ds(offset, tall)], dst_ref=row_ref.at[source],
            send_sem=line_send.at[source, k - 1], recv_sem=line_recv.at[source],
            device_id=(row, (col + k) % cols), device_id_type=MESH,
        )

    def lines(source):
        @pl.when(home == col)
        def _():
            for k in range(1, cols):
                line_copy(source, k).start()
            row_ref[source] = col_ref[source, :, pl.ds(offset, tall)]

    def routes(step):
        if step < steps - 1:
            return [(d, k) for k in range(cols) for d in (0, 1)]
        return [(2 * k // cols, k) for k in range(cols)]

    pieces[row, col] = standard(col)
    for direction, k in routes(0):
        if k > 0 and direction == routes(0)[2 * k][0]:
            swaps[k - 1].wait_recv()
        launch(ring_copy(direction, 0, k, row))
    assemble(row)
    launch(sib_copy(0, row))
    lines(row)
    waiting = [(0, sibling)]
    count = 1
    for step in range(steps):
        sources = (
            row_at((place + 2 * chips - step - 1) % chips, core, depth, width),
            row_at((place + step + 1) % chips, core, depth, width),
        )
        for direction, k in routes(step):
            ring_copy(direction, step, k, sources[direction]).wait_recv()
            if step + 1 < steps and (direction, k) in routes(step + 1):
                launch(ring_copy(direction, step + 1, k, sources[direction]))
        for source in sources if step < steps - 1 else sources[:1]:
            assemble(source)
            launch(sib_copy(count, source))
            lines(source)
            waiting.append((count, source + 1 - 2 * core))
            count += 1
        due = waiting[:-2] if step < steps - 1 else waiting
        waiting = waiting[len(due):]
        for index, source in due:
            sib_copy(index, source).wait_recv()
            lines(source)

    block = col_ref.shape[1]
    product = lax.dot_general(
        phenos_ref[...], col_ref[...].reshape(rows * block, wide),
        (((1,), (1,)), ((), ())), preferred_element_type=jnp.float32,
    )
    parts[0] = product
    trades = []
    for k in range(1, cols):
        trade = pltpu.make_async_remote_copy(
            src_ref=parts.at[0], dst_ref=parts.at[k],
            send_sem=part_send.at[k - 1], recv_sem=part_recv.at[k - 1],
            device_id=(row, (col + k) % cols), device_id_type=MESH,
        )
        trade.start()
        trades.append(trade)

    @pl.when(home != col)
    def _():
        def take(source, carry):
            line_copy(source, 1).wait_recv()
            return carry
        lax.fori_loop(0, rows, take, 0)

    @pl.when(home == col)
    def _():
        def take(source, carry):
            for k in range(1, cols):
                line_copy(source, k).wait_send()
            return carry
        lax.fori_loop(0, rows, take, 0)

    total = parts[0]
    for k in range(1, cols):
        trades[k - 1].wait_recv()
        total = total + parts[k]
    weight_ref[...] = total
    for copy in sent + trades:
        copy.wait_send()


def product_kernel(row_ref, col_ref, weight_ref, grm_ref, projected_ref):
    sites = row_ref.shape[0]

    @pl.when(pl.program_id(0) == 2)
    def _():
        part = projected_ref.shape[1]
        col = lax.axis_index("col")
        lane = pl.ds(pl.multiple_of(col * part, 128), part)
        projected_ref[...] = jnp.dot(
            weight_ref[...], row_ref[:, lane].astype(jnp.float32),
            precision=lax.Precision.HIGHEST, preferred_element_type=jnp.float32,
        ) * (1.0 / sites)

    tall = grm_ref.shape[0]
    lines = pl.ds(pl.multiple_of(pl.program_id(0) * tall, 128), tall)
    grm_ref[...] = lax.dot_general(
        row_ref[:, lines], col_ref[...], (((0,), (0,)), ((), ())),
        preferred_element_type=jnp.float32,
    ) * (1.0 / sites)


def per_device(rows, cols, dosage, phenos):
    sites, samples = dosage.shape
    count = phenos.shape[0]
    block, wide, tall = sites * cols, samples // cols, samples // rows
    total = rows * block
    vmem = pl.BlockSpec(memory_space=pltpu.VMEM)
    dma = pltpu.SemaphoreType.DMA
    chips = rows // 2
    others = cols - 1
    col_block, row_block, weight = pl.pallas_call(
        functools.partial(gather_kernel, rows, cols),
        out_shape=[
            jax.ShapeDtypeStruct((rows, block, wide), jnp.bfloat16),
            jax.ShapeDtypeStruct((rows, block, tall), jnp.bfloat16),
            jax.ShapeDtypeStruct((count, total), jnp.float32),
        ],
        in_specs=[vmem, vmem],
        out_specs=[vmem, vmem, vmem],
        scratch_shapes=[
            pltpu.VMEM((others, sites, wide), jnp.bfloat16),
            pltpu.VMEM((rows, cols, sites, wide), jnp.bfloat16),
            pltpu.VMEM((cols, count, total), jnp.float32),
            dma((others,)), dma((others,)),
            dma((2, chips // 2, cols)), dma((2, chips // 2, cols)),
            dma((chips,)), dma((chips,)),
            dma((rows, others)), dma((rows,)),
            dma((others,)), dma((others,)),
        ],
        compiler_params=pltpu.CompilerParams(
            collective_id=0, has_side_effects=True, vmem_limit_bytes=48 * 2**20
        ),
        name="gather",
    )(dosage, phenos)
    row_block = row_block.reshape(total, tall)
    col_block = col_block.reshape(total, wide)
    lines = 128
    grm, projected = pl.pallas_call(
        product_kernel,
        grid=(tall // lines,),
        out_shape=[
            jax.ShapeDtypeStruct((tall, wide), jnp.float32),
            jax.ShapeDtypeStruct((count, tall // cols), jnp.float32),
        ],
        in_specs=[vmem, vmem, vmem],
        out_specs=[
            pl.BlockSpec((lines, wide), lambda i: (i, 0)),
            pl.BlockSpec((count, tall // cols), lambda i: (0, 0)),
        ],
        compiler_params=pltpu.CompilerParams(vmem_limit_bytes=48 * 2**20),
        name="product",
    )(row_block, col_block, weight)
    return grm, projected


def solution(mesh):
    rows, cols = mesh.shape["row"], mesh.shape["col"]
    return jax.shard_map(
        functools.partial(per_device, rows, cols),
        mesh=mesh,
        in_specs=(P(("row", "col"), None), P(None, "col")),
        out_specs=(P("row", "col"), P(None, ("row", "col"))),
        check_vma=False,
    )
```
